32 devices in a mesh: group: 2 (over y), beam: 4 (over z), fft: 2 (over x), sub: 2 (over core).
Axes of the slice: x: 2, y: 2, z: 4, core: 2. Of those that a mesh axis runs over, the one named last changes fastest.
Arguments:
- uv_grid: float32 [8, 2, 2048, 2048], P(('group', 'beam'), None, ('fft', 'sub')), parts along dimension 0, may hold values from -6 to 6
- beam_gain: float32 [8, 512, 512], P(('group', 'beam'), ('fft', 'sub')), parts along dimension 0, may hold values from 0.1 to 1
- sub_pixel: float32 [8, 2], P(('group', 'beam')), parts along dimension 0, may hold values from 0 to 1
- intersection_tiles: int32 [8, 4], P('group'), parts along dimension 0, may hold values from 0 to 7, as said below
- tile_offsets: int32 [8, 4, 2], P(('group', 'beam')), parts along dimension 0, may hold values from 0 to 252
Outputs:
- sky: float32 [16, 256, 256], P(('group', 'beam'), ('fft', 'sub')), parts along dimension 0
The draws below stay inside these ranges and needn't reach their ends.
There are 2 independent parts, one for each index of `group`. The reference program is written for one: setup_inputs(seed, part) draws one part's arguments, and reference() takes and returns one part's arrays. A program takes and returns all parts, laid end to end along the dimension named above; each array names one. Nothing has to cross between parts.
Inputs may be any that keep to these rules, and one draw needn't show every extreme that they name: `intersection_tiles`: each row names 4 distinct sky tiles; sky tile t belongs to owner t // 2, and the tiles of beam b belong to owners b - 1 to b + 2 taken modulo the number of owners, with at most 2 of them on one owner.
All inputs are finite; a program needn't handle non-finite values.
Results may differ from the reference program's by a relative error of at most 0.0037.
Values may be sent and summed in bfloat16 or wider, within the bound.
A program may use at most 64 MiB of HBM per device.

```python
import math
import jax
import jax.numpy as jnp
from jax import lax

NG = 2048
W = 512
S = 256
K = 4
TILE_DEV = 2
BEAMS = 4
TILES = 8


def draw_intersection_tiles(key, part):
    owners = TILES // TILE_DEV
    full = jax.random.randint(jax.random.fold_in(key, 11), (BEAMS,), 0, 4)
    keys = jax.random.split(jax.random.fold_in(key, 12), BEAMS)
    others = jax.vmap(lambda k: jax.random.permutation(k, 3 * TILE_DEV)[:K - TILE_DEV])(keys)
    others = others + TILE_DEV * (others >= TILE_DEV * full[:, None]).astype(jnp.int32)
    paired = full[:, None] * TILE_DEV + jnp.arange(TILE_DEV, dtype=jnp.int32)[None, :]
    nearby = jnp.concatenate([paired, others], axis=1).astype(jnp.int32)
    distance = nearby // TILE_DEV - 1
    beams = jnp.arange(BEAMS, dtype=jnp.int32)[:, None]
    holder = jnp.mod(beams + distance, owners)
    return (holder * TILE_DEV + jnp.mod(nearby, TILE_DEV)).astype(jnp.int32)


def set_ends(drawn, key, smallest, largest):
    spot = [jax.random.randint(jax.random.fold_in(key, axis), (), 0, length) for axis, length in enumerate(drawn.shape)]
    longest = drawn.shape.index(max(drawn.shape))
    next_to = spot[:longest] + [(spot[longest] + 1) % drawn.shape[longest]] + spot[longest + 1:]
    return drawn.at[tuple(spot)].set(smallest).at[tuple(next_to)].set(largest)


def levels(own_key, dims, cuts, smallest, largest):
    def one(position, shards_of):
        heights = jax.random.uniform(jax.random.fold_in(jax.random.fold_in(own_key, 6), position), (shards_of,), jnp.float32, smallest / len(cuts), largest / len(cuts))
        return jnp.repeat(jnp.exp(heights), dims[position] // shards_of).reshape((-1,) + (1,) * (len(dims) - position - 1))

    factor_of = one(*cuts[0])
    for cut in cuts[1:]:
        factor_of = factor_of * one(*cut)
    return factor_of


def scatter_about(stream_key, dims, scale, reach, cuts=(), kind=jnp.bfloat16):
    values = scale * jax.random.normal(stream_key, dims, jnp.float32)
    if cuts:
        values = values * levels(stream_key, dims, cuts, -0.22, 0.18)
    return jnp.clip(values, -reach, reach).astype(kind)


def setup_inputs(seed: int = 0, part: int = 0) -> dict:
    key_of = jax.random.split(jax.random.key(seed), 6)
    part_splits = jax.random.split(jax.random.fold_in(key_of[5], part), 6)
    uv_grid = scatter_about(part_splits[0], (BEAMS, 2, NG, NG), 1.0, 6.0, ((0, 4), (2, 4)), jnp.float32)
    beam_gain = jnp.clip(jnp.exp(math.log(1.0) - 2.3025851 * jax.random.uniform(part_splits[1], (BEAMS, W, W), jnp.float32) ** levels(part_splits[1], (BEAMS, W, W), ((0, 4), (1, 4)), -0.2, 0.2)), 0.1, 1.0)
    sub_pixel = jnp.clip(1.0 * jax.random.uniform(part_splits[2], (BEAMS, 2), jnp.float32) ** levels(part_splits[2], (BEAMS, 2), ((0, 4),), -0.2, 0.2), 0.0, 1.0)
    intersection_tiles = draw_intersection_tiles(jax.random.fold_in(jax.random.fold_in(key_of[5], part), 71), part)
    tile_offsets = set_ends(jax.random.randint(part_splits[4], (BEAMS, K, 2), 0, W - S - 3), jax.random.fold_in(part_splits[4], 1), 0, (W - S - 3) - 1).astype(jnp.int32)
    return dict(uv_grid=uv_grid, beam_gain=beam_gain, sub_pixel=sub_pixel, intersection_tiles=intersection_tiles, tile_offsets=tile_offsets)


def phase_table(rows, cols, length):
    turns = jnp.mod(rows[:, None] * cols[None, :], length)
    angle = turns.astype(jnp.float32) * (2.0 * 3.141592653589793 / length)
    return jnp.cos(angle), jnp.sin(angle)


def kernel_weight(t):
    a = jnp.abs(t)
    near = (1.5 * a - 2.5) * a * a + 1.0
    far = ((-0.5 * a + 2.5) * a - 4.0) * a + 2.0
    return jnp.where(a <= 1.0, near, jnp.where(a < 2.0, far, 0.0 * a))


def interp(offset, frac, rows, cols):
    place = (offset + 1 + rows).astype(frac.dtype) + frac
    return kernel_weight(cols.astype(frac.dtype)[None, :] - place[:, None])


def reference(uv_grid, beam_gain, sub_pixel, intersection_tiles, tile_offsets):
    half = W // 2
    sky_cols = (jnp.arange(W) - half).astype(jnp.int32)
    freq = jnp.arange(NG).astype(jnp.int32)
    cos_u, sin_u = phase_table(freq, sky_cols, NG)
    cos_b = cos_u.astype(jnp.bfloat16)
    sin_b = sin_u.astype(jnp.bfloat16)
    columns = jnp.mod(sky_cols, NG)
    tile_rows = jnp.arange(S).astype(jnp.int32)
    image_index = jnp.arange(W).astype(jnp.int32)

    def one_beam(items):
        grid, gain, shift, offsets = items
        field = lax.complex(grid[0], grid[1])
        spectra = jnp.fft.ifft(field, axis=1)[:, columns] * NG
        real_b = jnp.real(spectra).astype(jnp.bfloat16)
        imag_b = jnp.imag(spectra).astype(jnp.bfloat16)
        image = (jnp.dot(cos_b.T, real_b, preferred_element_type=jnp.float32)
                 - jnp.dot(sin_b.T, imag_b, preferred_element_type=jnp.float32)) / NG
        stacked = jnp.stack([gain * image, gain * gain])
        down = jax.vmap(lambda off: interp(off, shift[0], tile_rows, image_index))(offsets[:, 0])
        across = jax.vmap(lambda off: interp(off, shift[1], tile_rows, image_index))(offsets[:, 1])
        left = jnp.einsum('kiy,cyx->kcix', down, stacked, precision=lax.Precision.HIGHEST)
        return jnp.einsum('kcix,kjx->kcij', left, across, precision=lax.Precision.HIGHEST)

    pieces = lax.map(one_beam, (uv_grid, beam_gain, sub_pixel, tile_offsets))
    sums = jax.ops.segment_sum(pieces.reshape(BEAMS * K, 2, S, S), intersection_tiles.reshape(-1), num_segments=TILES)
    return sums[:, 0] / jnp.maximum(sums[:, 1], 0.5)
```

```python
import functools

import jax
import jax.numpy as jnp
import ml_dtypes
import numpy as np
from jax import lax
from jax.experimental import pallas as pl
from jax.experimental.pallas import tpu as pltpu
from jax.sharding import PartitionSpec as P

S = 256
TILE_DEV = 2
RADIX = 4
HOPS = (1, -1, 2)
MESH = pl.DeviceIdType.MESH
F32 = jnp.float32
BF16 = jnp.bfloat16


def turns(rows, cols, length):
    angle = np.mod(np.outer(rows, cols), length) * (2.0 * np.pi / length)
    return np.cos(angle), np.sin(angle)


def column_tables(length, window):
    fold = length // RADIX
    per = window // RADIX
    tables = []
    for c in range(RADIX):
        cos, sin = turns(np.arange(fold), RADIX * np.arange(per) + c - window // 2, length)
        tables.append(np.concatenate([cos, sin], axis=1))
    full = np.stack(tables).astype(np.float32)
    high = full.astype(ml_dtypes.bfloat16)
    low = (full - high.astype(np.float32)).astype(ml_dtypes.bfloat16)
    return np.stack([high, low])


def row_tables(length, window, rows):
    cos, sin = turns(np.arange(window) - window // 2, np.arange(rows), length)
    return np.stack([cos, sin]).astype(np.float32).astype(ml_dtypes.bfloat16)


def near(a):
    return (1.5 * a - 2.5) * a * a + 1.0


def far(a):
    return ((-0.5 * a + 2.5) * a - 4.0) * a + 2.0


def taps(frac):
    return far(1.0 + frac), near(frac), near(1.0 - frac), far(2.0 - frac)


def member_index():
    return lax.axis_index("fft") * lax.axis_size("sub") + lax.axis_index("sub")


def dft_kernel(groups, quarter, step, uv_ref, col_ref, row_ref, part_ref, buf, spec, sems):
    rows = buf.shape[1]
    length = buf.shape[2]
    fold = length // RADIX
    window = spec.shape[1]
    per = window // RADIX
    chunks = rows // step

    def copy(i):
        span = pl.ds(pl.multiple_of(i * step, step), step)
        return pltpu.make_async_copy(uv_ref.at[0, :, span], buf.at[:, span], sems.at[i])

    for i in range(chunks):
        copy(i).start()

    def one(i, carry):
        copy(i).wait()
        start = pl.multiple_of(i * step, step)
        span = pl.ds(start, step)
        a = [buf[0, span, j * fold:(j + 1) * fold] for j in range(RADIX)]
        b = [buf[1, span, j * fold:(j + 1) * fold] for j in range(RADIX)]
        ap, am, aq, an = a[0] + a[2], a[0] - a[2], a[1] + a[3], a[1] - a[3]
        bp, bm, bq, bn = b[0] + b[2], b[0] - b[2], b[1] + b[3], b[1] - b[3]
        folded = (
            (ap + aq, bp + bq),
            (am - bn, bm + an),
            (ap - aq, bp - bq),
            (am + bn, bm - an),
        )
        for c in range(RADIX):
            z = jnp.concatenate(folded[c], axis=0)
            high = z.astype(BF16)
            low = (z - high.astype(F32)).astype(BF16)
            out = jnp.dot(high, col_ref[0, c], preferred_element_type=F32)
            out += jnp.dot(low, col_ref[0, c], preferred_element_type=F32)
            out += jnp.dot(high, col_ref[1, c], preferred_element_type=F32)
            real = out[:step, :per] - out[step:, per:]
            imag = out[:step, per:] + out[step:, :per]
            spec[span, c * per:(c + 1) * per] = real.astype(BF16)
            spec[pl.ds(pl.multiple_of(rows + i * step, step), step), c * per:(c + 1) * per] = imag.astype(BF16)
        return carry

    lax.fori_loop(0, chunks, one, 0)
    cos = row_ref[0].astype(F32)
    sin = row_ref[1].astype(F32)
    if quarter:
        place = lax.broadcasted_iota(jnp.int32, (window, 1), 0)
        turn = jnp.bitwise_and(member_index() * place, 3)
        plus = jnp.where(turn == 0, 1.0, jnp.where(turn == 2, -1.0, 0.0))
        cross = jnp.where(turn == 1, 1.0, jnp.where(turn == 3, -1.0, 0.0))
        cos, sin = plus * cos - cross * sin, cross * cos + plus * sin
    table = jnp.concatenate([cos.astype(BF16), (-sin).astype(BF16)], axis=1)
    image = jnp.dot(table, spec[...], preferred_element_type=F32) * (1.0 / length)
    wide = window // groups
    for g in range(groups):
        part_ref[g] = image[:, g * wide:(g + 1) * wide].astype(BF16)


def combine_kernel(
    groups, shift_ref, tiles_ref, offs_ref, part_ref, gain_ref, out_ref,
    gsend, grecv, precv, filt, nsend, nrecv, dsend, drecv, znsend, znrecv, zdsend, zdrecv,
    send_sems, recv_sems,
):
    me = member_index()
    owner = lax.axis_index("beam")
    owners = lax.axis_size("beam")
    subs = lax.axis_size("sub")
    own_rows = gain_ref.shape[1]
    window = gain_ref.shape[2]
    wide = window // groups
    per = window // RADIX
    side = S // groups
    count = offs_ref.shape[1]

    def member(other):
        return {"fft": other // subs, "sub": lax.rem(other, subs)}

    def beam(hop):
        return {"beam": lax.rem(owner + hop + owners, owners)}

    barrier = pltpu.get_barrier_semaphore()
    for d in range(1, groups):
        pl.semaphore_signal(barrier, inc=1, device_id=member(lax.rem(me + d, groups)), device_id_type=MESH)
    for hop in HOPS:
        pl.semaphore_signal(barrier, inc=1, device_id=beam(-hop), device_id_type=MESH)
    pl.semaphore_wait(barrier, groups - 1 + len(HOPS))

    def remote(src, dst, index, device):
        return pltpu.make_async_remote_copy(
            src_ref=src, dst_ref=dst, send_sem=send_sems.at[index], recv_sem=recv_sems.at[index],
            device_id=device, device_id_type=MESH)

    lanes = groups - 1
    peers = [(d, lax.rem(me + d, groups), lax.rem(me - d + groups, groups)) for d in range(1, groups)]
    part_copies = [remote(part_ref.at[to], precv.at[d - 1], d - 1, member(to)) for d, to, _ in peers]
    for c in part_copies:
        c.start()

    gain = gain_ref[0]
    source = lax.broadcasted_iota(jnp.int32, (window, window), 0)
    target = lax.broadcasted_iota(jnp.int32, (window, window), 1)
    natural = RADIX * lax.rem(target, per) + target // per
    order = jnp.where(source == natural, 1.0, 0.0).astype(BF16)
    high = gain.astype(BF16)
    rest = gain - high.astype(F32)
    middle = rest.astype(BF16)
    low = (rest - middle.astype(F32)).astype(BF16)
    moved = jnp.dot(high, order, preferred_element_type=F32)
    moved += jnp.dot(middle, order, preferred_element_type=F32)
    moved += jnp.dot(low, order, preferred_element_type=F32)
    for g in range(groups):
        gsend[g] = moved[:, g * wide:(g + 1) * wide]
    gain_copies = [remote(gsend.at[to], grecv.at[me], lanes + d - 1, member(to)) for d, to, _ in peers]
    for c in gain_copies:
        c.start()
    grecv[me] = gsend[me]

    image = part_ref[me].astype(F32)
    for (d, _, _), c in zip(peers, part_copies):
        c.wait_recv()
        image += precv[d - 1].astype(F32)
    for (d, to, frm), c in zip(peers, gain_copies):
        remote(gsend.at[to], grecv.at[frm], lanes + d - 1, member(to)).wait_recv()
    beam_gain = grecv[...].reshape(window, wide)
    down = taps(shift_ref[0, 0])
    across = taps(shift_ref[0, 1])

    def filter_rows(x):
        total = down[0] * x
        for d in range(1, 4):
            total += down[d] * pltpu.roll(x, window - d, 0)
        return total

    filt[0] = filter_rows(beam_gain * image)
    filt[1] = filter_rows(beam_gain * beam_gain)
    for k in range(count):
        top = offs_ref[0, k, 0]
        for g in range(groups):
            nsend[g, k] = filt[0, pl.ds(top + g * side, side), :].astype(BF16)
            dsend[g, k] = filt[1, pl.ds(top + g * side, side), :]
    num_copies = [remote(nsend.at[to], nrecv.at[me], 2 * lanes + d - 1, member(to)) for d, to, _ in peers]
    den_copies = [remote(dsend.at[to], drecv.at[me], 3 * lanes + d - 1, member(to)) for d, to, _ in peers]
    for c in den_copies + num_copies:
        c.start()
    nrecv[me] = nsend[me]
    drecv[me] = dsend[me]
    for d, to, frm in peers:
        remote(nsend.at[to], nrecv.at[frm], 2 * lanes + d - 1, member(to)).wait_recv()
        remote(dsend.at[to], drecv.at[frm], 3 * lanes + d - 1, member(to)).wait_recv()

    padded = S + 128
    column = lax.broadcasted_iota(jnp.int32, (window, padded), 0)
    column = RADIX * lax.rem(column, per) + column // per
    column = column - lax.broadcasted_iota(jnp.int32, (window, padded), 1)

    def filter_columns(x):
        total = across[0] * x
        for d in range(1, 4):
            total += across[d] * pltpu.roll(x, padded - d, 1)
        return total[:, :S]

    pieces = []
    for k in range(count):
        crop = jnp.where(column == offs_ref[0, k, 1], 1.0, 0.0).astype(BF16)
        num = jnp.concatenate([nrecv[g, k] for g in range(groups)], axis=1)
        den = jnp.concatenate([drecv[g, k] for g in range(groups)], axis=1)
        den_high = den.astype(BF16)
        den_low = (den - den_high.astype(F32)).astype(BF16)
        got = jnp.dot(jnp.concatenate([num, den_high, den_low], axis=0), crop, preferred_element_type=F32)
        pieces.append((filter_columns(got[:side]), filter_columns(got[side:2 * side] + got[2 * side:])))

    def owed(hop, slot):
        tile = lax.rem(owner + hop + owners, owners) * TILE_DEV + slot
        num = jnp.zeros((side, S), F32)
        den = jnp.zeros((side, S), F32)
        for k in range(count):
            take = jnp.where(tiles_ref[owner, k] == tile, 1.0, 0.0)
            num += take * pieces[k][0]
            den += take * pieces[k][1]
        return num, den

    base = 4 * lanes
    beam_copies = []
    for h, hop in enumerate(HOPS):
        for slot in range(TILE_DEV):
            num, den = owed(hop, slot)
            znsend[h, slot] = num.astype(BF16)
            zdsend[h, slot] = den
        pair = (
            remote(znsend.at[h], znrecv.at[h], base + h, beam(hop)),
            remote(zdsend.at[h], zdrecv.at[h], base + len(HOPS) + h, beam(hop)),
        )
        for c in pair:
            c.start()
        beam_copies.extend(pair)
    sums = [owed(0, slot) for slot in range(TILE_DEV)]
    for c in beam_copies:
        c.wait_recv()
    for slot in range(TILE_DEV):
        num, den = sums[slot]
        for h in range(len(HOPS)):
            num += znrecv[h, slot].astype(F32)
            den += zdrecv[h, slot]
        out_ref[slot] = num / jnp.maximum(den, 0.5)
    for c in part_copies + gain_copies + num_copies + den_copies + beam_copies:
        c.wait_send()


def body(uv_grid, beam_gain, sub_pixel, intersection_tiles, tile_offsets):
    groups = lax.axis_size(("fft", "sub"))
    rows = uv_grid.shape[2]
    length = uv_grid.shape[3]
    own_rows = beam_gain.shape[1]
    window = beam_gain.shape[2]
    wide = window // groups
    side = S // groups
    count = tile_offsets.shape[1]
    quarter = RADIX * rows == length
    if quarter:
        row_table = jnp.asarray(row_tables(length, window, rows))
    else:
        freq = member_index() * rows + jnp.arange(rows, dtype=jnp.int32)
        place = jnp.arange(window, dtype=jnp.int32) - window // 2
        angle = jnp.mod(place[:, None] * freq[None, :], length).astype(F32) * (2.0 * np.pi / length)
        row_table = jnp.stack([jnp.cos(angle), jnp.sin(angle)]).astype(BF16)
    step = min(128, rows)
    vmem = pl.BlockSpec(memory_space=pltpu.VMEM)
    smem = pl.BlockSpec(memory_space=pltpu.SMEM)
    part = pl.pallas_call(
        functools.partial(dft_kernel, groups, quarter, step),
        out_shape=jax.ShapeDtypeStruct((groups, window, wide), BF16),
        in_specs=[pl.BlockSpec(memory_space=pl.ANY), vmem, vmem],
        out_specs=vmem,
        scratch_shapes=[
            pltpu.VMEM((2, rows, length), F32),
            pltpu.VMEM((2 * rows, window), BF16),
            pltpu.SemaphoreType.DMA((rows // step,)),
        ],
    )(uv_grid, jnp.asarray(column_tables(length, window)), row_table)
    hops = len(HOPS)
    copies = 4 * (groups - 1) + 2 * hops
    return pl.pallas_call(
        functools.partial(combine_kernel, groups),
        out_shape=jax.ShapeDtypeStruct((TILE_DEV, side, S), F32),
        in_specs=[smem, smem, smem, vmem, vmem],
        out_specs=vmem,
        scratch_shapes=[
            pltpu.VMEM((groups, own_rows, wide), F32),
            pltpu.VMEM((groups, own_rows, wide), F32),
            pltpu.VMEM((groups - 1, window, wide), BF16),
            pltpu.VMEM((2, window, wide), F32),
            pltpu.VMEM((groups, count, side, wide), BF16),
            pltpu.VMEM((groups, count, side, wide), BF16),
            pltpu.VMEM((groups, count, side, wide), F32),
            pltpu.VMEM((groups, count, side, wide), F32),
            pltpu.VMEM((hops, TILE_DEV, side, S), BF16),
            pltpu.VMEM((hops, TILE_DEV, side, S), BF16),
            pltpu.VMEM((hops, TILE_DEV, side, S), F32),
            pltpu.VMEM((hops, TILE_DEV, side, S), F32),
            pltpu.SemaphoreType.DMA((copies,)),
            pltpu.SemaphoreType.DMA((copies,)),
        ],
        compiler_params=pltpu.CompilerParams(collective_id=0, has_side_effects=True),
    )(sub_pixel, intersection_tiles, tile_offsets, part, beam_gain)


def solution(mesh):
    placed = (
        P(("group", "beam"), None, ("fft", "sub"), None),
        P(("group", "beam"), ("fft", "sub"), None),
        P(("group", "beam"), None),
        P("group", None),
        P(("group", "beam"), None, None),
    )
    return jax.shard_map(
        body,
        mesh=mesh,
        in_specs=placed,
        out_specs=P(("group", "beam"), ("fft", "sub"), None),
        check_vma=False,
    )
```

```python
import functools

import jax
import jax.numpy as jnp
import ml_dtypes
import numpy as np
from jax import lax
from jax.experimental import pallas as pl
from jax.experimental.pallas import tpu as pltpu
from jax.sharding import PartitionSpec as P

S = 256
TILE_DEV = 2
RADIX = 4
HOPS = (1, -1, 2)
MESH = pl.DeviceIdType.MESH
F32 = jnp.float32
BF16 = jnp.bfloat16


def turns(rows, cols, length):
    angle = np.mod(np.outer(rows, cols), length) * (2.0 * np.pi / length)
    return np.cos(angle), np.sin(angle)


def column_tables(length, window):
    fold = length // RADIX
    per = window // RADIX
    tables = []
    for c in range(RADIX):
        cos, sin = turns(np.arange(fold), RADIX * np.arange(per) + c - window // 2, length)
        tables.append(np.concatenate([cos, sin], axis=1))
    full = np.stack(tables).astype(np.float32)
    high = full.astype(ml_dtypes.bfloat16)
    low = (full - high.astype(np.float32)).astype(ml_dtypes.bfloat16)
    return np.stack([high, low])


def row_tables(length, window, rows):
    cos, sin = turns(np.arange(window) - window // 2, np.arange(rows), length)
    return np.stack([cos, sin]).astype(np.float32).astype(ml_dtypes.bfloat16)


def near(a):
    return (1.5 * a - 2.5) * a * a + 1.0


def far(a):
    return ((-0.5 * a + 2.5) * a - 4.0) * a + 2.0


def taps(frac):
    return far(1.0 + frac), near(frac), near(1.0 - frac), far(2.0 - frac)


def kernel(
    groups, quarter, step, shift_ref, tiles_ref, offs_ref, gain_ref, uv_ref, col_hbm, row_hbm, out_ref,
    buf, col_ref, row_ref, table, spec, gsend, grecv, psend, precv, filt, crops,
    nsend, nrecv, dsend, drecv, znsend, znrecv, zdsend, zdrecv,
    load_sems, send_sems, recv_sems,
):
    chip, core = lax.axis_index("fft"), lax.axis_index("sub")
    chips, cores = lax.axis_size("fft"), lax.axis_size("sub")
    me = chip * cores + core
    owner = lax.axis_index("beam")
    owners = lax.axis_size("beam")
    rows, length = buf.shape[1], buf.shape[2]
    fold = length // RADIX
    window = gain_ref.shape[2]
    per = window // RADIX
    wide = window // groups
    side = S // groups
    count = offs_ref.shape[2]
    chunks = rows // step
    padded = crops.shape[2]

    def load(i):
        span = pl.ds(pl.multiple_of(i * step, step), step)
        return pltpu.make_async_copy(uv_ref.at[0, :, span], buf.at[:, span], load_sems.at[i])

    col_load = pltpu.make_async_copy(col_hbm, col_ref, load_sems.at[chunks])
    row_load = pltpu.make_async_copy(row_hbm, row_ref, load_sems.at[chunks + 1])
    row_load.start()
    col_load.start()
    for i in range(chunks):
        load(i).start()

    def beam(hop):
        return {"beam": lax.rem(owner + hop + owners, owners)}

    peers = []
    for a in list(range(1, chips)) + [0]:
        for e in range(cores):
            if a or e:
                to = (lax.rem(chip + a, chips), lax.rem(core + e, cores))
                frm = (lax.rem(chip - a + chips, chips), lax.rem(core - e + cores, cores))
                peers.append((
                    {"fft": to[0], "sub": to[1]}, to[0] * cores + to[1], frm[0] * cores + frm[1]))
    lanes = len(peers)

    barrier = pltpu.get_barrier_semaphore()
    for device, _, _ in peers:
        pl.semaphore_signal(barrier, inc=1, device_id=device, device_id_type=MESH)
    for hop in HOPS:
        pl.semaphore_signal(barrier, inc=1, device_id=beam(-hop), device_id_type=MESH)

    def remote(src, dst, index, device):
        return pltpu.make_async_remote_copy(
            src_ref=src, dst_ref=dst, send_sem=send_sems.at[index], recv_sem=recv_sems.at[index],
            device_id=device, device_id_type=MESH)

    def natural(place):
        return RADIX * jnp.bitwise_and(place, per - 1) + lax.shift_right_logical(place, per.bit_length() - 1)

    gain = gain_ref[0]
    source = lax.broadcasted_iota(jnp.int32, (window, window), 0)
    order = jnp.where(source == natural(lax.broadcasted_iota(jnp.int32, (1, window), 1)), 1.0, 0.0).astype(BF16)
    high = gain.astype(BF16)
    rest = gain - high.astype(F32)
    middle = rest.astype(BF16)
    low = (rest - middle.astype(F32)).astype(BF16)
    moved = jnp.dot(high, order, preferred_element_type=F32)
    moved += jnp.dot(middle, order, preferred_element_type=F32)
    moved += jnp.dot(low, order, preferred_element_type=F32)
    for g in range(groups):
        gsend[g] = moved[:, g * wide:(g + 1) * wide]

    pl.semaphore_wait(barrier, lanes + len(HOPS))
    gain_copies = [remote(gsend.at[to], grecv.at[me], i, device) for i, (device, to, _) in enumerate(peers)]
    for c in gain_copies:
        c.start()
    grecv[me] = gsend[me]

    row_load.wait()
    cos = row_ref[0].astype(F32)
    sin = row_ref[1].astype(F32)
    if quarter:
        turn = jnp.bitwise_and(me * lax.broadcasted_iota(jnp.int32, (window, 1), 0), 3)
        plus = jnp.where(turn == 0, 1.0, jnp.where(turn == 2, -1.0, 0.0))
        cross = jnp.where(turn == 1, 1.0, jnp.where(turn == 3, -1.0, 0.0))
        cos, sin = plus * cos - cross * sin, cross * cos + plus * sin
    table[:, :rows] = cos.astype(BF16)
    table[:, rows:] = (-sin).astype(BF16)

    down = taps(shift_ref[0, 0])
    across = taps(shift_ref[0, 1])

    def filter_rows(x):
        total = down[0] * x
        for d in range(1, 4):
            total += down[d] * pltpu.roll(x, window - d, 0)
        return total

    def filter_columns(x):
        total = across[0] * x
        for d in range(1, 4):
            total += across[d] * pltpu.roll(x, padded - d, 1)
        return total[:, :S]

    def columns(i, carry):
        load(i).wait()
        span = pl.ds(pl.multiple_of(i * step, step), step)
        a = [buf[0, span, j * fold:(j + 1) * fold] for j in range(RADIX)]
        b = [buf[1, span, j * fold:(j + 1) * fold] for j in range(RADIX)]
        ap, am, aq, an = a[0] + a[2], a[0] - a[2], a[1] + a[3], a[1] - a[3]
        bp, bm, bq, bn = b[0] + b[2], b[0] - b[2], b[1] + b[3], b[1] - b[3]
        folded = (
            (ap + aq, bp + bq),
            (am - bn, bm + an),
            (ap - aq, bp - bq),
            (am + bn, bm - an),
        )
        for c in range(RADIX):
            z = jnp.concatenate(folded[c], axis=0)
            high = z.astype(BF16)
            low = (z - high.astype(F32)).astype(BF16)
            out = jnp.dot(high, col_ref[0, c], preferred_element_type=F32)
            out += jnp.dot(low, col_ref[0, c], preferred_element_type=F32)
            out += jnp.dot(high, col_ref[1, c], preferred_element_type=F32)
            real = (out[:step, :per] - out[step:, per:]).astype(BF16)
            imag = (out[:step, per:] + out[step:, :per]).astype(BF16)
            for g in range(c * per // wide, (c + 1) * per // wide):
                at = g * wide - c * per
                spec[g, span] = real[:, at:at + wide]
                spec[g, pl.ds(pl.multiple_of(rows + i * step, step), step)] = imag[:, at:at + wide]
        return carry

    col_load.wait()
    lax.fori_loop(0, chunks // 2, columns, 0)

    for i, (device, to, frm) in enumerate(peers):
        remote(gsend.at[to], grecv.at[frm], i, device).wait_recv()
    beam_gain = grecv[...].reshape(window, wide)
    filt[1] = filter_rows(beam_gain * beam_gain)
    for k in range(count):
        top = offs_ref[0, 0, k]
        for g in range(groups):
            dsend[g, k] = filt[1, pl.ds(top + g * side, side), :]
    base = lanes
    den_copies = [
        remote(dsend.at[to], drecv.at[me], base + i, device) for i, (device, to, _) in enumerate(peers)]
    for c in den_copies:
        c.start()
    drecv[me] = dsend[me]

    lax.fori_loop(chunks // 2, chunks, columns, 0)

    base = 2 * lanes
    part_copies = []
    for i, (device, to, _) in enumerate(peers):
        share = jnp.dot(table[...], spec[to], preferred_element_type=F32) * (1.0 / length)
        psend[i] = share.astype(BF16)
        c = remote(psend.at[i], precv.at[i], base + i, device)
        c.start()
        part_copies.append(c)
    image = jnp.dot(table[...], spec[me], preferred_element_type=F32) * (1.0 / length)

    column = natural(lax.broadcasted_iota(jnp.int32, (window, 1), 0))
    target = lax.broadcasted_iota(jnp.int32, (window, padded), 1)
    for k in range(count):
        crops[k] = jnp.where(target == column - offs_ref[0, 1, k], 1.0, 0.0).astype(BF16)

    def owed(pieces, hop, slot):
        tile = lax.rem(owner + hop + owners, owners) * TILE_DEV + slot
        total = jnp.zeros((side, S), F32)
        for k in range(count):
            total += jnp.where(tiles_ref[owner, k] == tile, 1.0, 0.0) * pieces[k]
        return total

    for i, (device, to, frm) in enumerate(peers):
        remote(dsend.at[to], drecv.at[frm], lanes + i, device).wait_recv()
    pieces = []
    for k in range(count):
        den = jnp.concatenate([drecv[g, k] for g in range(groups)], axis=1)
        high = den.astype(BF16)
        low = (den - high.astype(F32)).astype(BF16)
        got = jnp.dot(jnp.concatenate([high, low], axis=0), crops[k], preferred_element_type=F32)
        pieces.append(filter_columns(got[:side] + got[side:]))
    base = 4 * lanes
    beam_copies = []
    for h, hop in enumerate(HOPS):
        for slot in range(TILE_DEV):
            zdsend[h, slot] = owed(pieces, hop, slot).astype(BF16)
        c = remote(zdsend.at[h], zdrecv.at[h], base + h, beam(hop))
        c.start()
        beam_copies.append(c)
    dens = [owed(pieces, 0, slot) for slot in range(TILE_DEV)]

    for i, c in enumerate(part_copies):
        c.wait_recv()
        image += precv[i].astype(F32)
    filt[0] = filter_rows(beam_gain * image)
    base = 3 * lanes
    num_copies = []
    for i, (device, to, _) in enumerate(peers):
        for k in range(count):
            nsend[to, k] = filt[0, pl.ds(offs_ref[0, 0, k] + to * side, side), :].astype(BF16)
        c = remote(nsend.at[to], nrecv.at[me], base + i, device)
        c.start()
        num_copies.append(c)
    for k in range(count):
        nrecv[me, k] = filt[0, pl.ds(offs_ref[0, 0, k] + me * side, side), :].astype(BF16)
    for i, (device, to, frm) in enumerate(peers):
        remote(nsend.at[to], nrecv.at[frm], base + i, device).wait_recv()

    pieces = []
    for k in range(count):
        num = jnp.concatenate([nrecv[g, k] for g in range(groups)], axis=1)
        pieces.append(filter_columns(jnp.dot(num, crops[k], preferred_element_type=F32)))
    base = 4 * lanes + len(HOPS)
    for h, hop in enumerate(HOPS):
        for slot in range(TILE_DEV):
            znsend[h, slot] = owed(pieces, hop, slot).astype(BF16)
        c = remote(znsend.at[h], znrecv.at[h], base + h, beam(hop))
        c.start()
        beam_copies.append(c)
    nums = [owed(pieces, 0, slot) for slot in range(TILE_DEV)]
    for c in beam_copies:
        c.wait_recv()
    for slot in range(TILE_DEV):
        num, den = nums[slot], dens[slot]
        for h in range(len(HOPS)):
            num += znrecv[h, slot].astype(F32)
            den += zdrecv[h, slot].astype(F32)
        out_ref[slot] = num / jnp.maximum(den, 0.5)
    for c in gain_copies + den_copies + part_copies + num_copies + beam_copies:
        c.wait_send()


def body(uv_grid, beam_gain, sub_pixel, intersection_tiles, tile_offsets):
    groups = lax.axis_size(("fft", "sub"))
    rows = uv_grid.shape[2]
    length = uv_grid.shape[3]
    own_rows = beam_gain.shape[1]
    window = beam_gain.shape[2]
    wide = window // groups
    side = S // groups
    count = tile_offsets.shape[1]
    quarter = RADIX * rows == length
    if quarter:
        row_table = jnp.asarray(row_tables(length, window, rows))
    else:
        member = lax.axis_index("fft") * lax.axis_size("sub") + lax.axis_index("sub")
        freq = member * rows + jnp.arange(rows, dtype=jnp.int32)
        place = jnp.arange(window, dtype=jnp.int32) - window // 2
        angle = jnp.mod(place[:, None] * freq[None, :], length).astype(F32) * (2.0 * np.pi / length)
        row_table = jnp.stack([jnp.cos(angle), jnp.sin(angle)]).astype(BF16)
    col_table = jnp.asarray(column_tables(length, window))
    step = min(128, rows)
    vmem = pl.BlockSpec(memory_space=pltpu.VMEM)
    smem = pl.BlockSpec(memory_space=pltpu.SMEM)
    anywhere = pl.BlockSpec(memory_space=pl.ANY)
    hops = len(HOPS)
    copies = 4 * (groups - 1) + 2 * hops
    left = (groups, count, side, wide)
    owed = (hops, TILE_DEV, side, S)
    return pl.pallas_call(
        functools.partial(kernel, groups, quarter, step),
        out_shape=jax.ShapeDtypeStruct((TILE_DEV, side, S), F32),
        in_specs=[smem, smem, smem, vmem, anywhere, anywhere, anywhere],
        out_specs=vmem,
        scratch_shapes=[
            pltpu.VMEM((2, rows, length), F32),
            pltpu.VMEM(col_table.shape, BF16),
            pltpu.VMEM(row_table.shape, BF16),
            pltpu.VMEM((window, 2 * rows), BF16),
            pltpu.VMEM((groups, 2 * rows, wide), BF16),
            pltpu.VMEM((groups, own_rows, wide), F32),
            pltpu.VMEM((groups, own_rows, wide), F32),
            pltpu.VMEM((groups - 1, window, wide), BF16),
            pltpu.VMEM((groups - 1, window, wide), BF16),
            pltpu.VMEM((2, window, wide), F32),
            pltpu.VMEM((count, window, S + 128), BF16),
            pltpu.VMEM(left, BF16),
            pltpu.VMEM(left, BF16),
            pltpu.VMEM(left, F32),
            pltpu.VMEM(left, F32),
            pltpu.VMEM(owed, BF16),
            pltpu.VMEM(owed, BF16),
            pltpu.VMEM(owed, BF16),
            pltpu.VMEM(owed, BF16),
            pltpu.SemaphoreType.DMA((rows // step + 2,)),
            pltpu.SemaphoreType.DMA((copies,)),
            pltpu.SemaphoreType.DMA((copies,)),
        ],
        compiler_params=pltpu.CompilerParams(collective_id=0, has_side_effects=True),
    )(sub_pixel, intersection_tiles, jnp.swapaxes(tile_offsets, 1, 2), beam_gain, uv_grid, col_table, row_table)


def solution(mesh):
    placed = (
        P(("group", "beam"), None, ("fft", "sub"), None),
        P(("group", "beam"), ("fft", "sub"), None),
        P(("group", "beam"), None),
        P("group", None),
        P(("group", "beam"), None, None),
    )
    return jax.shard_map(
        body,
        mesh=mesh,
        in_specs=placed,
        out_specs=P(("group", "beam"), ("fft", "sub"), None),
        check_vma=False,
    )
```

```python
import functools

import jax
import jax.numpy as jnp
import ml_dtypes
import numpy as np
from jax import lax
from jax.experimental import pallas as pl
from jax.experimental.pallas import tpu as pltpu
from jax.sharding import PartitionSpec as P

S = 256
TILE_DEV = 2
RADIX = 4
HOPS = (1, -1, 2)
MESH = pl.DeviceIdType.MESH
F32 = jnp.float32
BF16 = jnp.bfloat16


def turns(rows, cols, length):
    angle = np.mod(np.outer(rows, cols), length) * (2.0 * np.pi / length)
    return np.cos(angle), np.sin(angle)


def column_tables(length, window):
    fold = length // RADIX
    per = window // RADIX
    tables = []
    for c in range(RADIX):
        cos, sin = turns(np.arange(fold), RADIX * np.arange(per) + c - window // 2, length)
        tables.append(np.concatenate([cos, sin], axis=1))
    full = np.stack(tables).astype(np.float32)
    high = full.astype(ml_dtypes.bfloat16)
    low = (full - high.astype(np.float32)).astype(ml_dtypes.bfloat16)
    return np.stack([high, low])


def row_tables(length, window, rows):
    cos, sin = turns(np.arange(window) - window // 2, np.arange(rows), length)
    return np.stack([cos, sin]).astype(np.float32).astype(ml_dtypes.bfloat16)


def near(a):
    return (1.5 * a - 2.5) * a * a + 1.0


def far(a):
    return ((-0.5 * a + 2.5) * a - 4.0) * a + 2.0


def taps(frac):
    return far(1.0 + frac), near(frac), near(1.0 - frac), far(2.0 - frac)


def kernel(
    groups, quarter, step, shift_ref, tiles_ref, offs_ref, gain_ref, uv_ref, col_hbm, row_hbm, out_ref,
    buf, col_ref, row_ref, table, spec, gall, hsend, hrecv, psend, precv, filt, squares, crops,
    nsend, nrecv, znsend, znrecv, zdsend, zdrecv,
    load_sems, send_sems, recv_sems,
):
    chip, core = lax.axis_index("fft"), lax.axis_index("sub")
    chips, cores = lax.axis_size("fft"), lax.axis_size("sub")
    me = chip * cores + core
    owner = lax.axis_index("beam")
    owners = lax.axis_size("beam")
    rows, length = buf.shape[1], buf.shape[2]
    fold = length // RADIX
    window = gain_ref.shape[2]
    per = window // RADIX
    wide = window // groups
    side = S // groups
    count = offs_ref.shape[2]
    chunks = rows // step
    padded = crops.shape[2]

    def load(i):
        span = pl.ds(pl.multiple_of(i * step, step), step)
        return pltpu.make_async_copy(uv_ref.at[0, :, span], buf.at[:, span], load_sems.at[i])

    col_load = pltpu.make_async_copy(col_hbm, col_ref, load_sems.at[chunks])
    row_load = pltpu.make_async_copy(row_hbm, row_ref, load_sems.at[chunks + 1])
    col_load.start()
    for i in range(chunks):
        load(i).start()
    row_load.start()

    def beam(hop):
        return {"beam": lax.rem(owner + hop + owners, owners)}

    peers = []
    for a in list(range(1, chips)) + [0]:
        for e in range(cores):
            if a or e:
                to = (lax.rem(chip + a, chips), lax.rem(core + e, cores))
                frm = (lax.rem(chip - a + chips, chips), lax.rem(core - e + cores, cores))
                peers.append((
                    {"fft": to[0], "sub": to[1]}, to[0] * cores + to[1], frm[0] * cores + frm[1]))
    lanes = len(peers)
    shared = 2 * lanes + 1

    barrier = pltpu.get_barrier_semaphore()
    for device, _, _ in peers:
        pl.semaphore_signal(barrier, inc=1, device_id=device, device_id_type=MESH)
    for hop in HOPS:
        pl.semaphore_signal(barrier, inc=1, device_id=beam(-hop), device_id_type=MESH)

    def remote(src, dst, index, device):
        return pltpu.make_async_remote_copy(
            src_ref=src, dst_ref=dst, send_sem=send_sems.at[index], recv_sem=recv_sems.at[index],
            device_id=device, device_id_type=MESH)

    def natural(place):
        return RADIX * jnp.bitwise_and(place, per - 1) + lax.shift_right_logical(place, per.bit_length() - 1)

    own_rows = gain_ref.shape[1]

    def rows_of(member):
        return gall.at[pl.ds(pl.multiple_of(member * own_rows, own_rows), own_rows)]

    def at(a, e):
        other = lax.rem(chip + a + chips, chips), lax.rem(core + e + cores, cores)
        return {"fft": other[0], "sub": other[1]}, other[0] * cores + other[1]

    def slot_of(a, e):
        return a * cores + e

    pl.semaphore_wait(barrier, lanes + len(HOPS))
    gain_copies = []
    for a in list(range(1, chips)) + [0]:
        for e in range(cores):
            if (a == 0) != (e == 0):
                gain_copies.append(remote(gain_ref.at[0], rows_of(me), slot_of(a, e), at(a, e)[0]))
    for c in gain_copies:
        c.start()
    gall[pl.ds(pl.multiple_of(me * own_rows, own_rows), own_rows), :] = gain_ref[0]

    row_load.wait()
    cos = row_ref[0].astype(F32)
    sin = row_ref[1].astype(F32)
    if quarter:
        turn = jnp.bitwise_and(me * lax.broadcasted_iota(jnp.int32, (window, 1), 0), 3)
        plus = jnp.where(turn == 0, 1.0, jnp.where(turn == 2, -1.0, 0.0))
        cross = jnp.where(turn == 1, 1.0, jnp.where(turn == 3, -1.0, 0.0))
        cos, sin = plus * cos - cross * sin, cross * cos + plus * sin
    table[:, :rows] = cos.astype(BF16)
    table[:, rows:] = (-sin).astype(BF16)

    down = taps(shift_ref[0, 0])
    across = taps(shift_ref[0, 1])

    def filter_rows(x):
        total = down[0] * x
        for d in range(1, 4):
            total += down[d] * pltpu.roll(x, window - d, 0)
        return total

    def filter_columns(x):
        total = across[0] * x
        for d in range(1, 4):
            total += across[d] * pltpu.roll(x, padded - d, 1)
        return total[:, :S]

    def columns(i, carry):
        load(i).wait()
        span = pl.ds(pl.multiple_of(i * step, step), step)
        a = [buf[0, span, j * fold:(j + 1) * fold] for j in range(RADIX)]
        b = [buf[1, span, j * fold:(j + 1) * fold] for j in range(RADIX)]
        ap, am, aq, an = a[0] + a[2], a[0] - a[2], a[1] + a[3], a[1] - a[3]
        bp, bm, bq, bn = b[0] + b[2], b[0] - b[2], b[1] + b[3], b[1] - b[3]
        folded = (
            (ap + aq, bp + bq),
            (am - bn, bm + an),
            (ap - aq, bp - bq),
            (am + bn, bm - an),
        )
        for c in range(RADIX):
            z = jnp.concatenate(folded[c], axis=0)
            high = z.astype(BF16)
            low = (z - high.astype(F32)).astype(BF16)
            out = jnp.dot(high, col_ref[0, c], preferred_element_type=F32)
            out += jnp.dot(low, col_ref[0, c], preferred_element_type=F32)
            out += jnp.dot(high, col_ref[1, c], preferred_element_type=F32)
            real = (out[:step, :per] - out[step:, per:]).astype(BF16)
            imag = (out[:step, per:] + out[step:, :per]).astype(BF16)
            for g in range(c * per // wide, (c + 1) * per // wide):
                at = g * wide - c * per
                spec[g, span] = real[:, at:at + wide]
                spec[g, pl.ds(pl.multiple_of(rows + i * step, step), step)] = imag[:, at:at + wide]
        return carry

    col_load.wait()
    lax.fori_loop(0, chunks // 2, columns, 0)
    for a in range(1, chips):
        remote(gain_ref.at[0], rows_of(at(-a, 0)[1]), slot_of(a, 0), at(a, 0)[0]).wait_recv()
        for e in range(1, cores):
            c = remote(rows_of(at(-a, 0)[1]), rows_of(at(-a, 0)[1]), slot_of(a, e), at(0, e)[0])
            c.start()
            gain_copies.append(c)
    lax.fori_loop(chunks // 2, chunks, columns, 0)

    def share(member):
        return jnp.dot(table[...], spec[member], preferred_element_type=F32) * (1.0 / length)

    base = lanes + 1
    part_copies = []
    core_copies = {}
    for e in range(1, cores):
        for a in list(range(1, chips)) + [0]:
            i = (e - 1) * chips + a
            hsend[i] = share(at(a, e)[1]).astype(BF16)
            c = remote(hsend.at[i], hrecv.at[i], base + i, at(0, e)[0])
            c.start()
            core_copies[a, e] = c
    base += (cores - 1) * chips
    for a in range(1, chips):
        total = share(at(a, 0)[1])
        for e in range(1, cores):
            core_copies[a, e].wait_recv()
            total += hrecv[(e - 1) * chips + a].astype(F32)
        psend[a - 1] = total.astype(BF16)
        c = remote(psend.at[a - 1], precv.at[a - 1], base + a - 1, at(a, 0)[0])
        c.start()
        part_copies.append(c)
    image = share(me)
    for e in range(1, cores):
        core_copies[0, e].wait_recv()
        image += hrecv[(e - 1) * chips].astype(F32)

    for a in range(chips):
        for e in range(1, cores):
            frm = at(-a, -e)[1]
            remote(rows_of(frm), rows_of(frm), slot_of(a, e), at(0, e)[0]).wait_recv()
    source = lax.broadcasted_iota(jnp.int32, (window, wide), 0)
    order = jnp.where(source == natural(me * wide + lax.broadcasted_iota(jnp.int32, (1, wide), 1)), 1.0, 0.0)
    order = order.astype(BF16)
    gain = gall[...]
    high = gain.astype(BF16)
    low = (gain - high.astype(F32)).astype(BF16)
    beam_gain = jnp.dot(high, order, preferred_element_type=F32) + jnp.dot(low, order, preferred_element_type=F32)

    column = natural(lax.broadcasted_iota(jnp.int32, (window, 1), 0))
    target = lax.broadcasted_iota(jnp.int32, (window, padded), 1)
    for k in range(count):
        crops[k] = jnp.where(target == column - offs_ref[0, 1, k], 1.0, 0.0).astype(BF16)

    def owed(pieces, hop, slot):
        tile = lax.rem(owner + hop + owners, owners) * TILE_DEV + slot
        total = jnp.zeros((side, S), F32)
        for k in range(count):
            total += jnp.where(tiles_ref[owner, k] == tile, 1.0, 0.0) * pieces[k]
        return total

    pieces = []
    for q in range(window // 128):
        g = gall[:, q * 128:(q + 1) * 128]
        squares[q] = filter_rows(g * g)
    place = lax.broadcasted_iota(jnp.int32, (window, 1), 0)
    for k in range(count):
        den = jnp.concatenate(
            [squares[q, pl.ds(offs_ref[0, 0, k] + me * side, side), :] for q in range(window // 128)], axis=1)
        high = den.astype(BF16)
        low = (den - high.astype(F32)).astype(BF16)
        crop = jnp.where(target == place - offs_ref[0, 1, k], 1.0, 0.0).astype(BF16)
        got = jnp.dot(jnp.concatenate([high, low], axis=0), crop, preferred_element_type=F32)
        pieces.append(filter_columns(got[:side] + got[side:]))
    base = shared
    beam_copies = []
    for h, hop in enumerate(HOPS):
        for slot in range(TILE_DEV):
            zdsend[h, slot] = owed(pieces, hop, slot).astype(BF16)
        c = remote(zdsend.at[h], zdrecv.at[h], base + h, beam(hop))
        c.start()
        beam_copies.append(c)
    dens = [owed(pieces, 0, slot) for slot in range(TILE_DEV)]

    for i, c in enumerate(part_copies):
        c.wait_recv()
        image += precv[i].astype(F32)
    filt[...] = filter_rows(beam_gain * image)
    base = shared + 2 * len(HOPS)
    num_copies = []
    for i, (device, to, _) in enumerate(peers):
        for k in range(count):
            nsend[to, k] = filt[pl.ds(offs_ref[0, 0, k] + to * side, side), :].astype(BF16)
        c = remote(nsend.at[to], nrecv.at[me], base + i, device)
        c.start()
        num_copies.append(c)
    for k in range(count):
        nrecv[me, k] = filt[pl.ds(offs_ref[0, 0, k] + me * side, side), :].astype(BF16)
    for i, (device, to, frm) in enumerate(peers):
        remote(nsend.at[to], nrecv.at[frm], base + i, device).wait_recv()

    pieces = []
    for k in range(count):
        num = jnp.concatenate([nrecv[g, k] for g in range(groups)], axis=1)
        pieces.append(filter_columns(jnp.dot(num, crops[k], preferred_element_type=F32)))
    base = shared + len(HOPS)
    for h, hop in enumerate(HOPS):
        for slot in range(TILE_DEV):
            znsend[h, slot] = owed(pieces, hop, slot).astype(BF16)
        c = remote(znsend.at[h], znrecv.at[h], base + h, beam(hop))
        c.start()
        beam_copies.append(c)
    nums = [owed(pieces, 0, slot) for slot in range(TILE_DEV)]
    for c in beam_copies:
        c.wait_recv()
    for slot in range(TILE_DEV):
        num, den = nums[slot], dens[slot]
        for h in range(len(HOPS)):
            num += znrecv[h, slot].astype(F32)
            den += zdrecv[h, slot].astype(F32)
        out_ref[slot] = num / jnp.maximum(den, 0.5)
    for c in gain_copies + list(core_copies.values()) + part_copies + num_copies + beam_copies:
        c.wait_send()


def body(uv_grid, beam_gain, sub_pixel, intersection_tiles, tile_offsets):
    groups = lax.axis_size(("fft", "sub"))
    rows = uv_grid.shape[2]
    length = uv_grid.shape[3]
    own_rows = beam_gain.shape[1]
    window = beam_gain.shape[2]
    wide = window // groups
    side = S // groups
    count = tile_offsets.shape[1]
    quarter = RADIX * rows == length
    if quarter:
        row_table = jnp.asarray(row_tables(length, window, rows))
    else:
        member = lax.axis_index("fft") * lax.axis_size("sub") + lax.axis_index("sub")
        freq = member * rows + jnp.arange(rows, dtype=jnp.int32)
        place = jnp.arange(window, dtype=jnp.int32) - window // 2
        angle = jnp.mod(place[:, None] * freq[None, :], length).astype(F32) * (2.0 * np.pi / length)
        row_table = jnp.stack([jnp.cos(angle), jnp.sin(angle)]).astype(BF16)
    col_table = jnp.asarray(column_tables(length, window))
    step = min(128, rows)
    vmem = pl.BlockSpec(memory_space=pltpu.VMEM)
    smem = pl.BlockSpec(memory_space=pltpu.SMEM)
    anywhere = pl.BlockSpec(memory_space=pl.ANY)
    hops = len(HOPS)
    copies = 3 * (groups - 1) + 1 + 2 * hops
    chips, cores = lax.axis_size("fft"), lax.axis_size("sub")
    left = (groups, count, side, wide)
    owed = (hops, TILE_DEV, side, S)
    return pl.pallas_call(
        functools.partial(kernel, groups, quarter, step),
        out_shape=jax.ShapeDtypeStruct((TILE_DEV, side, S), F32),
        in_specs=[smem, smem, smem, vmem, anywhere, anywhere, anywhere],
        out_specs=vmem,
        scratch_shapes=[
            pltpu.VMEM((2, rows, length), F32),
            pltpu.VMEM(col_table.shape, BF16),
            pltpu.VMEM(row_table.shape, BF16),
            pltpu.VMEM((window, 2 * rows), BF16),
            pltpu.VMEM((groups, 2 * rows, wide), BF16),
            pltpu.VMEM((window, window), F32),
            pltpu.VMEM(((cores - 1) * chips, window, wide), BF16),
            pltpu.VMEM(((cores - 1) * chips, window, wide), BF16),
            pltpu.VMEM((chips - 1, window, wide), BF16),
            pltpu.VMEM((chips - 1, window, wide), BF16),
            pltpu.VMEM((window, wide), F32),
            pltpu.VMEM((window // 128, window, 128), F32),
            pltpu.VMEM((count, window, S + 128), BF16),
            pltpu.VMEM(left, BF16),
            pltpu.VMEM(left, BF16),
            pltpu.VMEM(owed, BF16),
            pltpu.VMEM(owed, BF16),
            pltpu.VMEM(owed, BF16),
            pltpu.VMEM(owed, BF16),
            pltpu.SemaphoreType.DMA((rows // step + 2,)),
            pltpu.SemaphoreType.DMA((copies,)),
            pltpu.SemaphoreType.DMA((copies,)),
        ],
        compiler_params=pltpu.CompilerParams(collective_id=0, has_side_effects=True),
    )(sub_pixel, intersection_tiles, jnp.swapaxes(tile_offsets, 1, 2), beam_gain, uv_grid, col_table, row_table)


def solution(mesh):
    placed = (
        P(("group", "beam"), None, ("fft", "sub"), None),
        P(("group", "beam"), ("fft", "sub"), None),
        P(("group", "beam"), None),
        P("group", None),
        P(("group", "beam"), None, None),
    )
    return jax.shard_map(
        body,
        mesh=mesh,
        in_specs=placed,
        out_specs=P(("group", "beam"), ("fft", "sub"), None),
        check_vma=False,
    )
```

```python
import functools

import jax
import jax.numpy as jnp
import ml_dtypes
import numpy as np
from jax import lax
from jax.experimental import pallas as pl
from jax.experimental.pallas import tpu as pltpu
from jax.sharding import PartitionSpec as P

S = 256
TILE_DEV = 2
RADIX = 4
HOPS = (1, -1, 2)
MESH = pl.DeviceIdType.MESH
F32 = jnp.float32
BF16 = jnp.bfloat16


def turns(rows, cols, length):
    angle = np.mod(np.outer(rows, cols), length) * (2.0 * np.pi / length)
    return np.cos(angle), np.sin(angle)


def column_tables(length, window):
    fold = length // RADIX
    per = window // RADIX
    tables = []
    for c in range(RADIX):
        cos, sin = turns(np.arange(fold), RADIX * np.arange(per) + c - window // 2, length)
        tables.append(np.concatenate([cos, sin], axis=1))
    full = np.stack(tables).astype(np.float32)
    high = full.astype(ml_dtypes.bfloat16)
    low = (full - high.astype(np.float32)).astype(ml_dtypes.bfloat16)
    return np.stack([high, low])


def row_tables(length, window, rows):
    cos, sin = turns(np.arange(window) - window // 2, np.arange(rows), length)
    return np.stack([cos, sin]).astype(np.float32).astype(ml_dtypes.bfloat16)


def near(a):
    return (1.5 * a - 2.5) * a * a + 1.0


def far(a):
    return ((-0.5 * a + 2.5) * a - 4.0) * a + 2.0


def taps(frac):
    return far(1.0 + frac), near(frac), near(1.0 - frac), far(2.0 - frac)


def kernel(
    groups, quarter, step, shift_ref, tiles_ref, offs_ref, gain_ref, uv_ref, col_hbm, row_hbm, out_ref,
    buf, col_ref, row_ref, table, spec, gall, hsend, hrecv, psend, precv, filt, squares, crops,
    nsend, nrecv, znsend, znrecv, zdsend, zdrecv,
    load_sems, send_sems, recv_sems,
):
    chip, core = lax.axis_index("fft"), lax.axis_index("sub")
    chips, cores = lax.axis_size("fft"), lax.axis_size("sub")
    me = chip * cores + core
    owner = lax.axis_index("beam")
    owners = lax.axis_size("beam")
    rows, length = buf.shape[1], buf.shape[2]
    fold = length // RADIX
    window = gain_ref.shape[2]
    per = window // RADIX
    wide = window // groups
    side = S // groups
    count = offs_ref.shape[2]
    chunks = rows // step
    padded = crops.shape[2]

    def load(i):
        span = pl.ds(pl.multiple_of(i * step, step), step)
        return pltpu.make_async_copy(uv_ref.at[0, :, span], buf.at[:, span], load_sems.at[i])

    col_load = pltpu.make_async_copy(col_hbm, col_ref, load_sems.at[chunks])
    row_load = pltpu.make_async_copy(row_hbm, row_ref, load_sems.at[chunks + 1])
    col_load.start()
    for i in range(chunks):
        load(i).start()
    row_load.start()

    def beam(hop):
        return {"beam": lax.rem(owner + hop + owners, owners)}

    peers = []
    for a in list(range(1, chips)) + [0]:
        for e in range(cores):
            if a or e:
                to = (lax.rem(chip + a, chips), lax.rem(core + e, cores))
                frm = (lax.rem(chip - a + chips, chips), lax.rem(core - e + cores, cores))
                peers.append((
                    {"fft": to[0], "sub": to[1]}, to[0] * cores + to[1], frm[0] * cores + frm[1]))
    lanes = len(peers)
    shared = 2 * lanes + 1

    barrier = pltpu.get_barrier_semaphore()
    for device, _, _ in peers:
        pl.semaphore_signal(barrier, inc=1, device_id=device, device_id_type=MESH)
    for hop in HOPS:
        pl.semaphore_signal(barrier, inc=1, device_id=beam(-hop), device_id_type=MESH)

    def remote(src, dst, index, device):
        return pltpu.make_async_remote_copy(
            src_ref=src, dst_ref=dst, send_sem=send_sems.at[index], recv_sem=recv_sems.at[index],
            device_id=device, device_id_type=MESH)

    def natural(place):
        return RADIX * jnp.bitwise_and(place, per - 1) + lax.shift_right_logical(place, per.bit_length() - 1)

    own_rows = gain_ref.shape[1]

    def rows_of(member):
        return gall.at[pl.ds(pl.multiple_of(member * own_rows, own_rows), own_rows)]

    def at(a, e):
        other = lax.rem(chip + a + chips, chips), lax.rem(core + e + cores, cores)
        return {"fft": other[0], "sub": other[1]}, other[0] * cores + other[1]

    def slot_of(a, e):
        return a * cores + e

    pl.semaphore_wait(barrier, lanes + len(HOPS))
    gain_copies = []
    for a in list(range(1, chips)) + [0]:
        for e in range(cores):
            if (a == 0) != (e == 0):
                gain_copies.append(remote(gain_ref.at[0], rows_of(me), slot_of(a, e), at(a, e)[0]))
    for c in gain_copies:
        c.start()
    gall[pl.ds(pl.multiple_of(me * own_rows, own_rows), own_rows), :] = gain_ref[0]

    down = taps(shift_ref[0, 0])
    across = taps(shift_ref[0, 1])

    def filter_rows(x):
        total = down[0] * x
        for d in range(1, 4):
            total += down[d] * pltpu.roll(x, window - d, 0)
        return total

    def filter_columns(x):
        total = across[0] * x
        for d in range(1, 4):
            total += across[d] * pltpu.roll(x, padded - d, 1)
        return total[:, :S]

    def columns(i, carry):
        load(i).wait()
        span = pl.ds(pl.multiple_of(i * step, step), step)
        a = [buf[0, span, j * fold:(j + 1) * fold] for j in range(RADIX)]
        b = [buf[1, span, j * fold:(j + 1) * fold] for j in range(RADIX)]
        ap, am, aq, an = a[0] + a[2], a[0] - a[2], a[1] + a[3], a[1] - a[3]
        bp, bm, bq, bn = b[0] + b[2], b[0] - b[2], b[1] + b[3], b[1] - b[3]
        folded = (
            (ap + aq, bp + bq),
            (am - bn, bm + an),
            (ap - aq, bp - bq),
            (am + bn, bm - an),
        )
        for c in range(RADIX):
            z = jnp.concatenate(folded[c], axis=0)
            high = z.astype(BF16)
            low = (z - high.astype(F32)).astype(BF16)
            out = jnp.dot(high, col_ref[0, c], preferred_element_type=F32)
            out += jnp.dot(low, col_ref[0, c], preferred_element_type=F32)
            out += jnp.dot(high, col_ref[1, c], preferred_element_type=F32)
            real = (out[:step, :per] - out[step:, per:]).astype(BF16)
            imag = (out[:step, per:] + out[step:, :per]).astype(BF16)
            for g in range(c * per // wide, (c + 1) * per // wide):
                at = g * wide - c * per
                spec[g, span] = real[:, at:at + wide]
                spec[g, pl.ds(pl.multiple_of(rows + i * step, step), step)] = imag[:, at:at + wide]
        return carry

    col_load.wait()
    lax.fori_loop(0, chunks // 2, columns, 0)
    row_load.wait()
    cos = row_ref[0].astype(F32)
    sin = row_ref[1].astype(F32)
    if quarter:
        turn = jnp.bitwise_and(me * lax.broadcasted_iota(jnp.int32, (window, 1), 0), 3)
        plus = jnp.where(turn == 0, 1.0, jnp.where(turn == 2, -1.0, 0.0))
        cross = jnp.where(turn == 1, 1.0, jnp.where(turn == 3, -1.0, 0.0))
        cos, sin = plus * cos - cross * sin, cross * cos + plus * sin
    table[:, :rows] = cos.astype(BF16)
    table[:, rows:] = (-sin).astype(BF16)
    lax.fori_loop(chunks // 2, chunks, columns, 0)

    def share(member):
        return jnp.dot(table[...], spec[member], preferred_element_type=F32) * (1.0 / length)

    base = lanes + 1
    part_copies = []
    core_copies = {}
    for e in range(1, cores):
        for a in list(range(1, chips)) + [0]:
            i = (e - 1) * chips + a
            hsend[i] = share(at(a, e)[1]).astype(BF16)
            c = remote(hsend.at[i], hrecv.at[i], base + i, at(0, e)[0])
            c.start()
            core_copies[a, e] = c
    base += (cores - 1) * chips
    for a in range(1, chips):
        total = share(at(a, 0)[1])
        for e in range(1, cores):
            core_copies[a, e].wait_recv()
            total += hrecv[(e - 1) * chips + a].astype(F32)
        psend[a - 1] = total.astype(BF16)
        c = remote(psend.at[a - 1], precv.at[a - 1], base + a - 1, at(a, 0)[0])
        c.start()
        part_copies.append(c)
    for a in range(1, chips):
        remote(gain_ref.at[0], rows_of(at(-a, 0)[1]), slot_of(a, 0), at(a, 0)[0]).wait_recv()
        for e in range(1, cores):
            c = remote(rows_of(at(-a, 0)[1]), rows_of(at(-a, 0)[1]), slot_of(a, e), at(0, e)[0])
            c.start()
            gain_copies.append(c)
    image = share(me)
    for e in range(1, cores):
        core_copies[0, e].wait_recv()
        image += hrecv[(e - 1) * chips].astype(F32)

    column = natural(lax.broadcasted_iota(jnp.int32, (window, 1), 0))
    target = lax.broadcasted_iota(jnp.int32, (window, padded), 1)
    for k in range(count):
        crops[k] = jnp.where(target == column - offs_ref[0, 1, k], 1.0, 0.0).astype(BF16)

    for a in range(chips):
        for e in range(1, cores):
            frm = at(-a, -e)[1]
            remote(rows_of(frm), rows_of(frm), slot_of(a, e), at(0, e)[0]).wait_recv()
    source = lax.broadcasted_iota(jnp.int32, (window, wide), 0)
    order = jnp.where(source == natural(me * wide + lax.broadcasted_iota(jnp.int32, (1, wide), 1)), 1.0, 0.0)
    order = order.astype(BF16)
    gain = gall[...]
    high = gain.astype(BF16)
    low = (gain - high.astype(F32)).astype(BF16)
    beam_gain = jnp.dot(high, order, preferred_element_type=F32) + jnp.dot(low, order, preferred_element_type=F32)

    def owed(pieces, hop, slot):
        tile = lax.rem(owner + hop + owners, owners) * TILE_DEV + slot
        total = jnp.zeros((side, S), F32)
        for k in range(count):
            total += jnp.where(tiles_ref[owner, k] == tile, 1.0, 0.0) * pieces[k]
        return total

    pieces = []
    for q in range(window // 128):
        g = gall[:, q * 128:(q + 1) * 128]
        squares[q] = filter_rows(g * g)
    place = lax.broadcasted_iota(jnp.int32, (window, 1), 0)
    for k in range(count):
        den = jnp.concatenate(
            [squares[q, pl.ds(offs_ref[0, 0, k] + me * side, side), :] for q in range(window // 128)], axis=1)
        high = den.astype(BF16)
        low = (den - high.astype(F32)).astype(BF16)
        crop = jnp.where(target == place - offs_ref[0, 1, k], 1.0, 0.0).astype(BF16)
        got = jnp.dot(jnp.concatenate([high, low], axis=0), crop, preferred_element_type=F32)
        pieces.append(filter_columns(got[:side] + got[side:]))
    base = shared
    beam_copies = []
    for h, hop in enumerate(HOPS):
        for slot in range(TILE_DEV):
            zdsend[h, slot] = owed(pieces, hop, slot).astype(BF16)
        c = remote(zdsend.at[h], zdrecv.at[h], base + h, beam(hop))
        c.start()
        beam_copies.append(c)
    dens = [owed(pieces, 0, slot) for slot in range(TILE_DEV)]

    for i, c in enumerate(part_copies):
        c.wait_recv()
        image += precv[i].astype(F32)
    filt[...] = filter_rows(beam_gain * image)
    base = shared + 2 * len(HOPS)
    num_copies = []
    for i, (device, to, _) in enumerate(peers):
        for k in range(count):
            nsend[to, k] = filt[pl.ds(offs_ref[0, 0, k] + to * side, side), :].astype(BF16)
        c = remote(nsend.at[to], nrecv.at[me], base + i, device)
        c.start()
        num_copies.append(c)
    for k in range(count):
        nrecv[me, k] = filt[pl.ds(offs_ref[0, 0, k] + me * side, side), :].astype(BF16)
    for i, (device, to, frm) in enumerate(peers):
        remote(nsend.at[to], nrecv.at[frm], base + i, device).wait_recv()

    pieces = []
    for k in range(count):
        num = jnp.concatenate([nrecv[g, k] for g in range(groups)], axis=1)
        pieces.append(filter_columns(jnp.dot(num, crops[k], preferred_element_type=F32)))
    base = shared + len(HOPS)
    for h, hop in enumerate(HOPS):
        for slot in range(TILE_DEV):
            znsend[h, slot] = owed(pieces, hop, slot).astype(BF16)
        c = remote(znsend.at[h], znrecv.at[h], base + h, beam(hop))
        c.start()
        beam_copies.append(c)
    nums = [owed(pieces, 0, slot) for slot in range(TILE_DEV)]
    for c in beam_copies:
        c.wait_recv()
    for slot in range(TILE_DEV):
        num, den = nums[slot], dens[slot]
        for h in range(len(HOPS)):
            num += znrecv[h, slot].astype(F32)
            den += zdrecv[h, slot].astype(F32)
        out_ref[slot] = num / jnp.maximum(den, 0.5)
    for c in gain_copies + list(core_copies.values()) + part_copies + num_copies + beam_copies:
        c.wait_send()


def body(uv_grid, beam_gain, sub_pixel, intersection_tiles, tile_offsets):
    groups = lax.axis_size(("fft", "sub"))
    rows = uv_grid.shape[2]
    length = uv_grid.shape[3]
    own_rows = beam_gain.shape[1]
    window = beam_gain.shape[2]
    wide = window // groups
    side = S // groups
    count = tile_offsets.shape[1]
    quarter = RADIX * rows == length
    if quarter:
        row_table = jnp.asarray(row_tables(length, window, rows))
    else:
        member = lax.axis_index("fft") * lax.axis_size("sub") + lax.axis_index("sub")
        freq = member * rows + jnp.arange(rows, dtype=jnp.int32)
        place = jnp.arange(window, dtype=jnp.int32) - window // 2
        angle = jnp.mod(place[:, None] * freq[None, :], length).astype(F32) * (2.0 * np.pi / length)
        row_table = jnp.stack([jnp.cos(angle), jnp.sin(angle)]).astype(BF16)
    col_table = jnp.asarray(column_tables(length, window))
    step = min(128, rows)
    vmem = pl.BlockSpec(memory_space=pltpu.VMEM)
    smem = pl.BlockSpec(memory_space=pltpu.SMEM)
    anywhere = pl.BlockSpec(memory_space=pl.ANY)
    hops = len(HOPS)
    copies = 3 * (groups - 1) + 1 + 2 * hops
    chips, cores = lax.axis_size("fft"), lax.axis_size("sub")
    left = (groups, count, side, wide)
    owed = (hops, TILE_DEV, side, S)
    return pl.pallas_call(
        functools.partial(kernel, groups, quarter, step),
        out_shape=jax.ShapeDtypeStruct((TILE_DEV, side, S), F32),
        in_specs=[smem, smem, smem, vmem, anywhere, anywhere, anywhere],
        out_specs=vmem,
        scratch_shapes=[
            pltpu.VMEM((2, rows, length), F32),
            pltpu.VMEM(col_table.shape, BF16),
            pltpu.VMEM(row_table.shape, BF16),
            pltpu.VMEM((window, 2 * rows), BF16),
            pltpu.VMEM((groups, 2 * rows, wide), BF16),
            pltpu.VMEM((window, window), F32),
            pltpu.VMEM(((cores - 1) * chips, window, wide), BF16),
            pltpu.VMEM(((cores - 1) * chips, window, wide), BF16),
            pltpu.VMEM((chips - 1, window, wide), BF16),
            pltpu.VMEM((chips - 1, window, wide), BF16),
            pltpu.VMEM((window, wide), F32),
            pltpu.VMEM((window // 128, window, 128), F32),
            pltpu.VMEM((count, window, S + 128), BF16),
            pltpu.VMEM(left, BF16),
            pltpu.VMEM(left, BF16),
            pltpu.VMEM(owed, BF16),
            pltpu.VMEM(owed, BF16),
            pltpu.VMEM(owed, BF16),
            pltpu.VMEM(owed, BF16),
            pltpu.SemaphoreType.DMA((rows // step + 2,)),
            pltpu.SemaphoreType.DMA((copies,)),
            pltpu.SemaphoreType.DMA((copies,)),
        ],
        compiler_params=pltpu.CompilerParams(collective_id=0, has_side_effects=True),
    )(sub_pixel, intersection_tiles, jnp.swapaxes(tile_offsets, 1, 2), beam_gain, uv_grid, col_table, row_table)


def solution(mesh):
    placed = (
        P(("group", "beam"), None, ("fft", "sub"), None),
        P(("group", "beam"), ("fft", "sub"), None),
        P(("group", "beam"), None),
        P("group", None),
        P(("group", "beam"), None, None),
    )
    return jax.shard_map(
        body,
        mesh=mesh,
        in_specs=placed,
        out_specs=P(("group", "beam"), ("fft", "sub"), None),
        check_vma=False,
    )
```
